32 devices in a mesh: dp: 16 (over z, y, x), mp: 2 (over core).
Axes of the slice: x: 2, y: 2, z: 4, core: 2. Of those that a mesh axis runs over, the one named last changes fastest.
Arguments:
- block_input: float32 [16384, 768], P('dp'), may hold values from -6 to 6
- slot_step: int32 [128], P('dp'), may hold values from 0 to 999, as said below
- block_group: int32 [64], P('dp'), may hold values from 0 to 1
- step_table: bfloat16 [1000, 768], replicated, may hold values from -3 to 3
- attn_gain: bfloat16 [768], replicated, may hold values from 0.5 to 1.5
- attn_shift: bfloat16 [768], replicated, may hold values from -3 to 3
- query_weight: bfloat16 [768, 768], P(None, 'mp'), may hold values from -0.21875 to 0.21875
- key_weight: bfloat16 [768, 768], P(None, 'mp'), may hold values from -0.21875 to 0.21875
- value_weight: bfloat16 [768, 768], P(None, 'mp'), may hold values from -0.21875 to 0.21875
- query_bias: bfloat16 [768], P('mp'), may hold values from -3 to 3
- value_bias: bfloat16 [768], P('mp'), may hold values from -3 to 3
- out_weight: bfloat16 [768, 768], P('mp'), may hold values from -2.5 to 2.5
- out_bias: bfloat16 [768], replicated, may hold values from -3 to 3
- mlp_gain: bfloat16 [768], replicated, may hold values from 0.5 to 1.5
- mlp_shift: bfloat16 [768], replicated, may hold values from -3 to 3
- up_weight: bfloat16 [768, 3072], P(None, 'mp'), may hold values from -0.21875 to 0.21875
- up_bias: bfloat16 [3072], P('mp'), may hold values from -3 to 3
- down_weight: bfloat16 [3072, 768], P('mp'), may hold values from -0.109375 to 0.109375
- down_bias: bfloat16 [768], replicated, may hold values from -3 to 3
- cotangent: float32 [16384, 768], P('dp'), may hold values from -6 to 6
Outputs:
- block_output: float32 [16384, 768], P(('dp', 'mp'))
- input_grad: float32 [16384, 768], P(('dp', 'mp'))
- table_grad: float32 [1000, 768], P('mp')
- attn_gain_grad: float32 [768], P('mp')
- attn_shift_grad: float32 [768], P('mp')
- query_weight_grad: float32 [768, 768], P(None, 'mp')
- key_weight_grad: float32 [768, 768], P(None, 'mp')
- value_weight_grad: float32 [768, 768], P(None, 'mp')
- query_bias_grad: float32 [768], P('mp')
- value_bias_grad: float32 [768], P('mp')
- out_weight_grad: float32 [768, 768], P('mp')
- out_bias_grad: float32 [768], P('mp')
- mlp_gain_grad: float32 [768], P('mp')
- mlp_shift_grad: float32 [768], P('mp')
- up_weight_grad: float32 [768, 3072], P(None, 'mp')
- up_bias_grad: float32 [3072], P('mp')
- down_weight_grad: float32 [3072, 768], P('mp')
- down_bias_grad: float32 [768], P('mp')
The draws below stay inside these ranges and needn't reach their ends.
Inputs may be any that keep to these rules, and one draw needn't show every extreme that they name: `slot_step`: both slots of a block whose block_group is 1 carry the same timestep.
All inputs are finite; a program needn't handle non-finite values.
Results may differ from the reference program's by a relative error of at most 0.012.
The reference program's roundings to bfloat16 on the way count: a program that leaves them out, or rounds other values in their place, can miss the bound.
Values may be sent and summed in bfloat16 or wider, within the bound.
No kernel may reach another device: no remote copies, remote signals or barrier semaphores. Data moves between devices by JAX's collectives and lax.ppermute only.
A program may use at most 128 MiB of HBM per device.

```python
import math
import jax
import jax.numpy as jnp
from jax import lax

D = 768
HEADS = 12
HEAD_DIM = 64
FF = 3072
STEPS = 1000
HALF = 128
BLOCK = 256
BLOCKS = 64
SLOTS = 128
TOKENS = 16384


def common_layout(key):
    base_key = jax.random.fold_in(key, 7)
    key_group, key_step, key_high, key_lowest = jax.random.split(base_key, 4)
    groups = jax.random.randint(key_group, (BLOCKS,), 0, 2)
    step_pairs = jax.random.randint(key_step, (BLOCKS, 2), 0, STEPS)
    high_block = jax.random.randint(key_high, (), 0, BLOCKS)
    lowest_block = (high_block + 1 + jax.random.randint(key_lowest, (), 0, BLOCKS - 1)) % BLOCKS
    block_index = jnp.arange(BLOCKS)
    step_pairs = jnp.where((block_index == high_block)[:, None], STEPS - 1, step_pairs)
    step_pairs = jnp.where((block_index == lowest_block)[:, None], 0, step_pairs)
    step_pairs = jnp.where((groups == 1)[:, None], step_pairs[:, :1], step_pairs)
    return (groups.astype(jnp.int32), step_pairs.reshape(SLOTS).astype(jnp.int32))


def draw_slot_step(key, part):
    return common_layout(key)[1]


def draw_block_group(key, part):
    return common_layout(key)[0]


def block_levels(own_key, dims, pieces, smallest, top_value):
    def one(axis_at, blocks):
        steps = jax.random.uniform(jax.random.fold_in(jax.random.fold_in(own_key, 6), axis_at), (blocks,), jnp.float32, smallest / len(pieces), top_value / len(pieces))
        return jnp.repeat(jnp.exp(steps), dims[axis_at] // blocks).reshape((-1,) + (1,) * (len(dims) - axis_at - 1))

    level = one(*pieces[0])
    for cut in pieces[1:]:
        level = level * one(*cut)
    return level


def scatter_about(own_key, extent, deviation, bound, shards=(), held_as=jnp.bfloat16):
    result = jax.random.normal(own_key, extent, jnp.float32) * deviation
    if len(shards) > 0:
        result = block_levels(own_key, extent, shards, -0.22, 0.18) * result
    return jnp.clip(result, min=-bound, max=bound).astype(held_as)


def setup_inputs(seed: int = 0) -> dict:
    seeds = jax.random.split(jax.random.key(seed), 21)
    return {
        "block_input": scatter_about(seeds[0], (TOKENS, D), 1.0, 6.0, ((0, 16),), jnp.float32),
        "slot_step": draw_slot_step(jax.random.fold_in(seeds[20], 71), 0),
        "block_group": draw_block_group(jax.random.fold_in(seeds[20], 71), 0),
        "step_table": scatter_about(seeds[3], (STEPS, D), 0.5, 3.0),
        "attn_gain": jnp.clip(1.0 + 0.1 * jax.random.normal(seeds[4], (D,), jnp.float32), 0.5, 1.5).astype(jnp.bfloat16),
        "attn_shift": scatter_about(seeds[5], (D,), 0.5, 3.0),
        "query_weight": scatter_about(seeds[6], (D, D), D ** -0.5, 0.21875, ((1, 2),)),
        "key_weight": scatter_about(seeds[7], (D, D), D ** -0.5, 0.21875, ((1, 2),)),
        "value_weight": scatter_about(seeds[8], (D, D), D ** -0.5, 0.21875, ((1, 2),)),
        "query_bias": scatter_about(seeds[9], (D,), 0.5, 3.0, ((0, 2),)),
        "value_bias": scatter_about(seeds[10], (D,), 0.5, 3.0, ((0, 2),)),
        "out_weight": scatter_about(seeds[11], (D, D), (D * 2 // BLOCK) ** -0.5, 2.5, ((0, 2),)),
        "out_bias": scatter_about(seeds[12], (D,), 0.5, 3.0),
        "mlp_gain": jnp.clip(1.0 + 0.1 * jax.random.normal(seeds[13], (D,), jnp.float32), 0.5, 1.5).astype(jnp.bfloat16),
        "mlp_shift": scatter_about(seeds[14], (D,), 0.5, 3.0),
        "up_weight": scatter_about(seeds[15], (D, FF), D ** -0.5, 0.21875, ((1, 2),)),
        "up_bias": scatter_about(seeds[16], (FF,), 0.5, 3.0, ((0, 2),)),
        "down_weight": scatter_about(seeds[17], (FF, D), FF ** -0.5, 0.109375, ((0, 2),)),
        "down_bias": scatter_about(seeds[18], (D,), 0.5, 3.0),
        "cotangent": scatter_about(seeds[19], (TOKENS, D), 1.0, 6.0, ((0, 16),), jnp.float32),
    }


@jax.custom_vjp
def low(v):
    return lax.optimization_barrier(v.astype(jnp.bfloat16)).astype(jnp.float32)

@jax.custom_vjp
def low_back(v):
    return v

def low_keep(v):
    return (low(v), None)

def low_pass(kept, grad):
    return (grad,)

def back_keep(v):
    return (v, None)

def back_low(kept, grad):
    return (low(grad),)
low.defvjp(low_keep, low_pass)
low_back.defvjp(back_keep, back_low)

def layer_norm(values, gain_row, shift_row):
    center = values - lax.optimization_barrier(jnp.mean(values, axis=-1, keepdims=True))
    spread = lax.optimization_barrier(jnp.mean(center * center, axis=-1, keepdims=True))
    return center * lax.rsqrt(spread + 1e-05) * gain_row + shift_row

def matmul_high(left, right):
    return jnp.dot(left, right, precision=lax.Precision.HIGHEST)

def group_forward(params_all, inputs_group, steps_group, kinds_group):
    step_table, attn_gain, attn_shift, query_weight, key_weight, value_weight, query_bias, value_bias, out_weight, out_bias, mlp_gain, mlp_shift, up_weight, up_bias, down_weight, down_bias = params_all
    count_blocks = kinds_group.shape[0]
    time_rows = jnp.take(step_table, steps_group, axis=0)
    start_res = (inputs_group.reshape(2 * count_blocks, HALF, D) + time_rows[:, None, :]).reshape(count_blocks * BLOCK, D)
    attn_low = low(layer_norm(start_res, attn_gain, attn_shift))
    head_shape = (count_blocks, BLOCK, HEADS, HEAD_DIM)
    queries = low(low_back(matmul_high(attn_low, query_weight) + query_bias)).reshape(head_shape)
    keys_low = low(low_back(matmul_high(attn_low, key_weight))).reshape(head_shape)
    values_low = low(low_back(matmul_high(attn_low, value_weight) + value_bias)).reshape(head_shape)
    positions = jnp.arange(BLOCK) // HALF
    allowed = (positions[:, None] == positions[None, :])[None] | (kinds_group[:, None, None] == 1)
    mask_bias = jnp.where(allowed, 0.0, -1000000000.0)[:, None]
    scores = jnp.einsum('bqhd,bkhd->bhqk', queries, keys_low, precision=lax.Precision.HIGHEST) * HEAD_DIM ** (-0.5) + mask_bias
    scores = low_back(scores)
    probs = low(jax.nn.softmax(scores, axis=-1))
    mixed = jnp.einsum('bhqk,bkhd->bqhd', probs, values_low, precision=lax.Precision.HIGHEST).reshape(count_blocks * BLOCK, D)
    mixed = low(low_back(mixed))
    middle = start_res + low_back(matmul_high(mixed, out_weight)) + out_bias
    mlp_low = low(layer_norm(middle, mlp_gain, mlp_shift))
    hidden_in = low_back(matmul_high(mlp_low, up_weight) + up_bias)
    hidden_low = low(jax.nn.gelu(hidden_in, approximate=True))
    return middle + low_back(matmul_high(hidden_low, down_weight)) + down_bias

def forward_all(params_all, block_input, slot_step, block_group):
    group_size = math.gcd(BLOCKS, 16)
    rounds_total = BLOCKS // group_size
    inputs_grouped = block_input.reshape(rounds_total, group_size * BLOCK, D)
    steps_grouped = slot_step.reshape(rounds_total, 2 * group_size)
    kinds_grouped = block_group.reshape(rounds_total, group_size)

    def one_round(carry, items):
        return (carry, group_forward(params_all, items[0], items[1], items[2]))
    carry_end, outputs = lax.scan(jax.checkpoint(one_round), jnp.zeros((), jnp.float32), (inputs_grouped, steps_grouped, kinds_grouped))
    return outputs.reshape(TOKENS, D)

def reference(block_input, slot_step, block_group, step_table, attn_gain, attn_shift, query_weight, key_weight, value_weight, query_bias, value_bias, out_weight, out_bias, mlp_gain, mlp_shift, up_weight, up_bias, down_weight, down_bias, cotangent):
    params_all = tuple((weight_item.astype(jnp.float32) for weight_item in (step_table, attn_gain, attn_shift, query_weight, key_weight, value_weight, query_bias, value_bias, out_weight, out_bias, mlp_gain, mlp_shift, up_weight, up_bias, down_weight, down_bias)))

    def run_block(params_in, input_in):
        return forward_all(params_in, input_in, slot_step, block_group)
    block_output, pull_back = jax.vjp(run_block, params_all, block_input)
    param_grads, input_grad = pull_back(cotangent)
    return (block_output, input_grad, param_grads[0], param_grads[1], param_grads[2], param_grads[3], param_grads[4], param_grads[5], param_grads[6], param_grads[7], param_grads[8], param_grads[9], param_grads[10], param_grads[11], param_grads[12], param_grads[13], param_grads[14], param_grads[15])
```

```python
from functools import partial

import jax
import jax.numpy as jnp
from jax import lax
from jax.sharding import PartitionSpec as P

D = 768
HEAD_DIM = 64
STEPS = 1000
HALF = 128
BLOCK = 256


def product(left, right):
    return jnp.dot(left, right, preferred_element_type=jnp.float32)


def norm_parts(values, gain_row, shift_row):
    center = values - jnp.mean(values, axis=-1, keepdims=True)
    inverse = lax.rsqrt(jnp.mean(center * center, axis=-1, keepdims=True) + 1e-05)
    normed = center * inverse
    return (normed * gain_row + shift_row, normed, inverse)


def norm_back(grad_out, normed, inverse, gain_row):
    scaled = grad_out * gain_row
    return inverse * (
        scaled
        - jnp.mean(scaled, axis=-1, keepdims=True)
        - normed * jnp.mean(scaled * normed, axis=-1, keepdims=True)
    )


def swap_cores(values):
    return lax.ppermute(values, "mp", [(0, 1), (1, 0)])


def swap_bit(values, bit):
    size = lax.axis_size("dp")
    return lax.ppermute(values, "dp", [(i, i ^ (1 << bit)) for i in range(size)])


def add_low(left, right):
    return (left.astype(jnp.float32) + right.astype(jnp.float32)).astype(jnp.bfloat16)


def bit_orders():
    count = (lax.axis_size("dp") - 1).bit_length()
    first = [0, 2, 1] if count > 2 else list(range(count))
    second = [1, 2, 0] if count > 2 else list(range(count))
    return (first + list(range(len(first), count)), second + list(range(len(second), count)))


def sum_dp(values, order):
    index = lax.axis_index("dp")
    cuts = []
    for bit in order[:-1]:
        half = values.shape[0] // 2
        side = (index >> bit) & 1
        received = swap_bit(lax.dynamic_slice_in_dim(values, (1 - side) * half, half, 0), bit)
        values = add_low(lax.dynamic_slice_in_dim(values, side * half, half, 0), received)
        cuts.append((bit, side))
    values = add_low(values, swap_bit(values, order[-1]))
    for bit, side in reversed(cuts):
        received = swap_bit(values, bit)
        values = jnp.where(
            side == 0,
            jnp.concatenate([values, received], 0),
            jnp.concatenate([received, values], 0),
        )
    return values


def on_device(
    block_input,
    slot_step,
    block_group,
    step_table,
    attn_gain,
    attn_shift,
    query_weight,
    key_weight,
    value_weight,
    query_bias,
    value_bias,
    out_weight,
    out_bias,
    mlp_gain,
    mlp_shift,
    up_weight,
    up_bias,
    down_weight,
    down_bias,
    cotangent,
):
    tok_rows = block_input.shape[0]
    blocks_here = block_group.shape[0]
    heads_here = query_weight.shape[1] // HEAD_DIM
    scale = HEAD_DIM ** (-0.5)
    share_rows = tok_rows // lax.axis_size("mp")
    core = lax.axis_index("mp")
    row_begin = core * share_rows
    order_first, order_second = bit_orders()
    gain_first = attn_gain.astype(jnp.float32)
    gain_second = mlp_gain.astype(jnp.float32)

    def own_first(values):
        half = values.shape[0] // 2
        return jnp.concatenate(
            [
                lax.dynamic_slice_in_dim(values, core * half, half, 0),
                lax.dynamic_slice_in_dim(values, (1 - core) * half, half, 0),
            ],
            0,
        )

    def own_rows(values):
        return values[:share_rows]

    def scatter_rows(values):
        return values[:share_rows] + swap_cores(values[share_rows:].astype(jnp.bfloat16)).astype(
            jnp.float32
        )

    def gather_rows(values):
        return jnp.concatenate([values, swap_cores(values)], 0)

    block_input = own_first(block_input)
    slot_step = own_first(slot_step)
    block_group = own_first(block_group)
    cotangent = own_first(cotangent)

    def split_heads(values):
        return values.reshape(blocks_here, BLOCK, heads_here, HEAD_DIM)

    time_rows = jnp.take(step_table, slot_step, axis=0).astype(jnp.float32)
    start_res = (block_input.reshape(slot_step.shape[0], HALF, D) + time_rows[:, None, :]).reshape(
        tok_rows, D
    )
    attn_normed, attn_hat, attn_inverse = norm_parts(
        start_res, gain_first, attn_shift.astype(jnp.float32)
    )
    attn_low = attn_normed.astype(jnp.bfloat16)
    queries = (product(attn_low, query_weight) + query_bias.astype(jnp.float32)).astype(
        jnp.bfloat16
    )
    keys_low = product(attn_low, key_weight).astype(jnp.bfloat16)
    values_low = (product(attn_low, value_weight) + value_bias.astype(jnp.float32)).astype(
        jnp.bfloat16
    )
    positions = jnp.arange(BLOCK) // HALF
    allowed = (positions[:, None] == positions[None, :])[None] | (block_group[:, None, None] == 1)
    mask_bias = jnp.where(allowed, 0.0, -1000000000.0).astype(jnp.float32)[:, None]

    def score_blocks():
        return (
            jnp.einsum(
                "bqhd,bkhd->bhqk",
                split_heads(queries),
                split_heads(keys_low),
                preferred_element_type=jnp.float32,
            )
            * scale
            + mask_bias
        )

    scores = score_blocks()
    top_score = jnp.max(scores, axis=-1, keepdims=True)
    scores_exp = jnp.exp(scores - top_score)
    total_exp = jnp.sum(scores_exp, axis=-1, keepdims=True)
    log_total = top_score + jnp.log(total_exp)
    probs_low = (scores_exp / total_exp).astype(jnp.bfloat16)
    mixed = (
        jnp.einsum(
            "bhqk,bkhd->bqhd",
            probs_low,
            split_heads(values_low),
            preferred_element_type=jnp.float32,
        )
        .reshape(tok_rows, -1)
        .astype(jnp.bfloat16)
    )
    middle = (
        own_rows(start_res)
        + scatter_rows(product(mixed, out_weight))
        + out_bias.astype(jnp.float32)
    )
    mlp_normed, mlp_hat, mlp_inverse = norm_parts(
        middle, gain_second, mlp_shift.astype(jnp.float32)
    )
    mlp_low = gather_rows(mlp_normed.astype(jnp.bfloat16))
    hidden_in = product(mlp_low, up_weight) + up_bias.astype(jnp.float32)
    hidden_act, gelu_pull = jax.vjp(partial(jax.nn.gelu, approximate=True), hidden_in)
    hidden_low = hidden_act.astype(jnp.bfloat16)
    block_output = (
        middle
        + scatter_rows(product(hidden_low, down_weight))
        + down_bias.astype(jnp.float32)
    )
    cot_low = cotangent.astype(jnp.bfloat16)
    down_weight_grad = product(hidden_low.T, cot_low)
    pre_grad = gelu_pull(product(cot_low, down_weight.T))[0].astype(jnp.bfloat16)
    up_weight_grad = product(mlp_low.T, pre_grad)
    up_bias_grad = jnp.sum(pre_grad.astype(jnp.float32), axis=0)
    mlp_normed_grad = scatter_rows(product(pre_grad, up_weight.T))
    cot_own = own_rows(cotangent)
    middle_grad = cot_own + norm_back(mlp_normed_grad, mlp_hat, mlp_inverse, gain_second)
    middle_low = gather_rows(middle_grad.astype(jnp.bfloat16))
    out_weight_grad = product(mixed.T, middle_low)
    mixed_grad = product(middle_low, out_weight.T).astype(jnp.bfloat16)
    probs = jnp.exp(score_blocks() - log_total)
    value_grad = (
        jnp.einsum(
            "bhqk,bqhd->bkhd",
            probs.astype(jnp.bfloat16),
            split_heads(mixed_grad),
            preferred_element_type=jnp.float32,
        )
        .reshape(tok_rows, -1)
        .astype(jnp.bfloat16)
    )
    prob_grad = jnp.einsum(
        "bqhd,bkhd->bhqk",
        split_heads(mixed_grad),
        split_heads(values_low),
        preferred_element_type=jnp.float32,
    )
    score_grad = (probs * (prob_grad - jnp.sum(probs * prob_grad, axis=-1, keepdims=True))).astype(
        jnp.bfloat16
    )
    query_grad = (
        (
            jnp.einsum(
                "bhqk,bkhd->bqhd",
                score_grad,
                split_heads(keys_low),
                preferred_element_type=jnp.float32,
            )
            * scale
        )
        .reshape(tok_rows, -1)
        .astype(jnp.bfloat16)
    )
    key_grad = (
        (
            jnp.einsum(
                "bhqk,bqhd->bkhd",
                score_grad,
                split_heads(queries),
                preferred_element_type=jnp.float32,
            )
            * scale
        )
        .reshape(tok_rows, -1)
        .astype(jnp.bfloat16)
    )
    query_weight_grad = product(attn_low.T, query_grad)
    key_weight_grad = product(attn_low.T, key_grad)
    value_weight_grad = product(attn_low.T, value_grad)
    query_bias_grad = jnp.sum(query_grad.astype(jnp.float32), axis=0)
    value_bias_grad = jnp.sum(value_grad.astype(jnp.float32), axis=0)
    attn_normed_grad = scatter_rows(
        product(query_grad, query_weight.T)
        + product(key_grad, key_weight.T)
        + product(value_grad, value_weight.T)
    )
    attn_hat_own = own_rows(attn_hat)
    input_grad = middle_grad + norm_back(
        attn_normed_grad, attn_hat_own, own_rows(attn_inverse), gain_first
    )
    slot_count = share_rows // HALF
    slot_sums = jnp.sum(input_grad.reshape(slot_count, HALF, D), axis=1)

    down_low = down_weight_grad.astype(jnp.bfloat16)
    up_low = up_weight_grad.astype(jnp.bfloat16)
    projection_low = jnp.concatenate(
        [query_weight_grad, key_weight_grad, value_weight_grad], 1
    ).astype(jnp.bfloat16)
    out_low = out_weight_grad.astype(jnp.bfloat16)

    def two_ways(values):
        cut = values.shape[0] // 2
        return jnp.concatenate(
            [sum_dp(values[:cut], order_first), sum_dp(values[cut:], order_second)], 0
        ).astype(jnp.float32)

    down_weight_grad = two_ways(down_low)
    up_weight_grad = two_ways(up_low)
    projection_grad = two_ways(projection_low)
    query_weight_grad, key_weight_grad, value_weight_grad = jnp.split(projection_grad, 3, axis=1)

    own_vectors = jnp.stack(
        [
            jnp.sum(attn_normed_grad * attn_hat_own, axis=0),
            jnp.sum(attn_normed_grad, axis=0),
            jnp.sum(middle_grad, axis=0),
            jnp.sum(mlp_normed_grad * mlp_hat, axis=0),
            jnp.sum(mlp_normed_grad, axis=0),
            jnp.sum(cot_own, axis=0),
        ]
    )
    width = D // lax.axis_size("mp")
    peer_vectors = swap_cores(
        lax.dynamic_slice_in_dim(own_vectors, (1 - core) * width, width, 1)
    )
    shared_vectors = lax.dynamic_slice_in_dim(own_vectors, core * width, width, 1) + peer_vectors
    slots_both = own_first(gather_rows(slot_sums.astype(jnp.bfloat16)))
    slots_here = slot_step.shape[0]
    slots_all = lax.dynamic_update_slice_in_dim(
        jnp.zeros((slots_here * lax.axis_size("dp"), D), jnp.bfloat16),
        slots_both,
        lax.axis_index("dp") * slots_here,
        0,
    )
    steps_mine = own_first(slot_step)

    def spread(digits):
        return lax.dynamic_update_slice_in_dim(
            jnp.zeros((slots_all.shape[0],), jnp.float32),
            digits.astype(jnp.float32),
            lax.axis_index("dp") * slots_here,
            0,
        )

    vectors = jnp.concatenate(
        [
            shared_vectors.reshape(-1),
            query_bias_grad,
            value_bias_grad,
            up_bias_grad,
            spread(steps_mine // 32),
            spread(steps_mine % 32),
        ]
    )
    small = jnp.concatenate(
        [out_low, slots_all, jnp.pad(vectors, (0, 128 * D - vectors.shape[0])).reshape(128, D).astype(jnp.bfloat16)], 0
    )
    small = sum_dp(small, order_first)
    out_weight_grad = small[: out_low.shape[0]].astype(jnp.float32)
    slot_table = small[out_low.shape[0] : out_low.shape[0] + slots_all.shape[0]]
    vectors = small[out_low.shape[0] + slots_all.shape[0] :].astype(jnp.float32).reshape(-1)
    parts = []
    at = 0
    for size in [width] * 6 + [query_bias_grad.shape[0]] * 2 + [up_bias_grad.shape[0]] + [
        slots_all.shape[0]
    ] * 2:
        parts.append(vectors[at : at + size])
        at += size
    (
        attn_gain_grad,
        attn_shift_grad,
        out_bias_grad,
        mlp_gain_grad,
        mlp_shift_grad,
        down_bias_grad,
        query_bias_grad,
        value_bias_grad,
        up_bias_grad,
        steps_high,
        steps_low,
    ) = parts
    all_steps = (steps_high * 32.0 + steps_low).astype(jnp.int32)
    table_rows = STEPS // lax.axis_size("mp")
    one_hot = (
        (jnp.arange(table_rows) + core * table_rows)[:, None] == all_steps[None, :]
    ).astype(jnp.bfloat16)
    table_grad = product(one_hot, slot_table)
    return (
        block_output,
        input_grad,
        table_grad,
        attn_gain_grad,
        attn_shift_grad,
        query_weight_grad,
        key_weight_grad,
        value_weight_grad,
        query_bias_grad,
        value_bias_grad,
        out_weight_grad,
        out_bias_grad,
        mlp_gain_grad,
        mlp_shift_grad,
        up_weight_grad,
        up_bias_grad,
        down_weight_grad,
        down_bias_grad,
    )


def solution(mesh):
    return jax.shard_map(
        on_device,
        mesh=mesh,
        in_specs=(
            P("dp", None),
            P("dp"),
            P("dp"),
            P(),
            P(),
            P(),
            P(None, "mp"),
            P(None, "mp"),
            P(None, "mp"),
            P("mp"),
            P("mp"),
            P("mp", None),
            P(),
            P(),
            P(),
            P(None, "mp"),
            P("mp"),
            P("mp", None),
            P(),
            P("dp", None),
        ),
        out_specs=(
            P(("dp", "mp"), None),
            P(("dp", "mp"), None),
            P("mp", None),
            P("mp"),
            P("mp"),
            P(None, "mp"),
            P(None, "mp"),
            P(None, "mp"),
            P("mp"),
            P("mp"),
            P("mp", None),
            P("mp"),
            P("mp"),
            P("mp"),
            P(None, "mp"),
            P("mp"),
            P("mp", None),
            P("mp"),
        ),
        check_vma=False,
    )
```
